32 devices in a mesh: row: 4 (over y, x), col: 8 (over z, core).
Axes of the slice: x: 2, y: 2, z: 4, core: 2. Of those that a mesh axis runs over, the one named last changes fastest.
Arguments:
- tokens: bfloat16 [512, 5120], P('row'), may hold values from -6 to 6
- expert_ids: int32 [512], replicated, may hold values from 0 to 7
- modality: int32 [512], replicated, may hold values from 0 to 1
- tile_counts: int32 [2, 8], replicated, may hold values from 1 to 4, as said below
- router: bfloat16 [5120, 8], P(None, 'col'), may hold values from -0.15625 to 0.15625
- w_gate: bfloat16 [8, 5120, 4096], P('col', None, 'row'), may hold values from -0.078125 to 0.078125
- w_up: bfloat16 [8, 5120, 4096], P('col', None, 'row'), may hold values from -0.078125 to 0.078125
- w_down: bfloat16 [8, 4096, 5120], P('col', 'row'), may hold values from -0.09375 to 0.09375
- shared_gate: bfloat16 [5120, 8192], P('row', 'col'), may hold values from -0.078125 to 0.078125
- shared_up: bfloat16 [5120, 8192], P('row', 'col'), may hold values from -0.078125 to 0.078125
- shared_down: bfloat16 [8192, 5120], P('col', 'row'), may hold values from -0.0625 to 0.0625
Outputs:
- mixed: bfloat16 [512, 5120], P('col', 'row')
The draws below stay inside these ranges and needn't reach their ends.
Inputs may be any that keep to these rules, and one draw needn't show every extreme that they name: `tile_counts`: in every draw some expert's text segment has 4 tiles and at least 32 text tokens, and some expert's image segment has 4 tiles and at least 32 image tokens.
All inputs are finite; a program needn't handle non-finite values.
Results may differ from the reference program's by a relative error of at most 0.0052.
Values may be sent and summed in bfloat16 or wider, within the bound.
No kernel may reach another device: no remote copies, remote signals or barrier semaphores. Data moves between devices by JAX's collectives and lax.ppermute only.
A program may use at most 128 MiB of HBM per device.

```python
import jax
import jax.numpy as jnp
from jax import lax

D = 5120
FFW = 4096
FS = 8192
TILE = 8
MAXT = 4
TOKENS = 512
E = 8


def routing(key):
    base = jax.random.fold_in(key, 7)
    keys = jax.random.split(base, 6)
    weights = (2 ** jax.random.randint(keys[0], (E,), 0, 4)).astype(jnp.int32)
    bounds = jnp.cumsum(weights).astype(jnp.int32)
    picks = jax.random.randint(keys[1], (TOKENS,), 0, bounds[-1])
    chosen = jnp.sum((picks[:, None] >= bounds[None, :]).astype(jnp.int32), axis=1).astype(jnp.int32)
    flags = (jax.random.randint(keys[2], (TOKENS,), 0, 5) < 2).astype(jnp.int32)
    counts = jax.random.randint(keys[3], (2, E), 1, MAXT + 1).astype(jnp.int32)
    hottest = jax.random.randint(keys[4], (2,), 0, E).astype(jnp.int32)
    order = jax.random.permutation(keys[5], TOKENS)
    places = jnp.zeros((TOKENS,), jnp.int32).at[order].set(jnp.arange(TOKENS, dtype=jnp.int32))
    capacity = MAXT * TILE
    forced_text = places < capacity
    forced_image = (places >= capacity) & (places < 2 * capacity)
    chosen = jnp.where(forced_text, hottest[0], jnp.where(forced_image, hottest[1], chosen))
    flags = jnp.where(forced_text, 0, jnp.where(forced_image, 1, flags))
    counts = counts.at[0, hottest[0]].set(MAXT).at[1, hottest[1]].set(MAXT)
    return (chosen.astype(jnp.int32), flags.astype(jnp.int32), counts.astype(jnp.int32))


def draw_expert_ids(key, part):
    return routing(key)[0]


def draw_modality(key, part):
    return routing(key)[1]


def draw_tile_counts(key, part):
    return routing(key)[2]


def block_scale(own_key, dims, shards, low, high):
    factor_of = 1.0
    for axis_at, blocks in shards:
        heights = jax.random.uniform(jax.random.fold_in(jax.random.fold_in(own_key, 6), axis_at), (blocks,), jnp.float32, low / len(shards), high / len(shards))
        factor_of = factor_of * jnp.repeat(jnp.exp(heights), dims[axis_at] // blocks).reshape((-1,) + (1,) * (len(dims) - 1 - axis_at))
    return factor_of


def centred(stream_key, dims, deviation, most, cuts=(), kind=jnp.bfloat16):
    array = jax.random.normal(stream_key, dims, jnp.float32) * deviation
    if len(cuts) > 0:
        array = block_scale(stream_key, dims, cuts, -0.22, 0.18) * array
    return jnp.clip(array, min=-most, max=most).astype(kind)


def setup_inputs(seed: int = 0) -> dict:
    key_list = jax.random.split(jax.random.key(seed), 12)
    return {
        "tokens": centred(key_list[0], (TOKENS, D), 1.0, 6.0, ((0, 4),)),
        "expert_ids": draw_expert_ids(jax.random.fold_in(key_list[11], 71), 0),
        "modality": draw_modality(jax.random.fold_in(key_list[11], 71), 0),
        "tile_counts": draw_tile_counts(jax.random.fold_in(key_list[11], 71), 0),
        "router": centred(key_list[4], (D, E), (D // 4) ** -0.5, 0.15625, ((1, 8),)),
        "w_gate": centred(key_list[5], (E, D, FFW), D ** -0.5, 0.078125, ((0, 8), (2, 4))),
        "w_up": centred(key_list[6], (E, D, FFW), D ** -0.5, 0.078125, ((0, 8), (2, 4))),
        "w_down": centred(key_list[7], (E, FFW, D), FFW ** -0.5, 0.09375, ((0, 8), (1, 4))),
        "shared_gate": centred(key_list[8], (D, FS), D ** -0.5, 0.078125, ((0, 4), (1, 8))),
        "shared_up": centred(key_list[9], (D, FS), D ** -0.5, 0.078125, ((0, 4), (1, 8))),
        "shared_down": centred(key_list[10], (FS, D), FS ** -0.5, 0.0625, ((0, 8), (1, 4))),
    }


def slot_places(expert_ids, modality, tile_counts, expert):
    capacity = MAXT * TILE
    places = jnp.full(expert_ids.shape, -1, jnp.int32)
    for kind in range(2):
        member = ((expert_ids == expert) & (modality == kind)).astype(jnp.int32)
        rank = (jnp.cumsum(member, dtype=jnp.int32) - 1).astype(jnp.int32)
        limit = (tile_counts[kind, expert] * TILE).astype(jnp.int32)
        keep = (member == 1) & (rank < limit)
        places = jnp.where(keep, (kind * capacity + rank).astype(jnp.int32), places)
    return places


def slot_table(places):
    slots = lax.broadcasted_iota(jnp.int32, (2 * MAXT * TILE, places.shape[0]), 0)
    return (slots == places[None, :]).astype(jnp.bfloat16)


def place_rows(places, values):
    index = jnp.maximum(places, 0).astype(jnp.int32)
    rows = jnp.take(values, index, axis=0)
    return jnp.where((places >= 0)[:, None], rows, jnp.zeros_like(rows))


def reference(tokens, expert_ids, modality, tile_counts, router, w_gate, w_up, w_down, shared_gate, shared_up, shared_down):
    def one_expert(expert, routed):
        places = slot_places(expert_ids, modality, tile_counts, expert)
        table = slot_table(places)
        taken = jnp.dot(table, tokens, preferred_element_type=jnp.float32).astype(jnp.bfloat16)
        column = lax.dynamic_slice_in_dim(router, expert, 1, 1)
        score = jax.nn.sigmoid(jnp.dot(taken, column, preferred_element_type=jnp.float32))
        scaled = (taken.astype(jnp.float32) * score).astype(jnp.bfloat16)
        gate = jnp.dot(scaled, w_gate[expert], preferred_element_type=jnp.float32)
        upper = jnp.dot(scaled, w_up[expert], preferred_element_type=jnp.float32)
        hidden = (jax.nn.silu(gate) * upper).astype(jnp.bfloat16)
        result = jnp.dot(hidden, w_down[expert], preferred_element_type=jnp.float32)
        return routed + place_rows(places, result)

    routed = lax.fori_loop(0, E, one_expert, jnp.zeros((TOKENS, D), jnp.float32))
    shared_gate_sum = jnp.dot(tokens, shared_gate, preferred_element_type=jnp.float32)
    shared_up_sum = jnp.dot(tokens, shared_up, preferred_element_type=jnp.float32)
    shared_hidden = (jax.nn.silu(shared_gate_sum) * shared_up_sum).astype(jnp.bfloat16)
    shared = jnp.dot(shared_hidden, shared_down, preferred_element_type=jnp.float32)
    return (routed + shared).astype(jnp.bfloat16)
```

```python
import jax
import jax.numpy as jnp
from jax import lax
from jax.sharding import PartitionSpec as P

TILE = 8
MAXT = 4


def slot_places(expert_ids, modality, tile_counts, expert):
    capacity = MAXT * TILE
    places = jnp.full(expert_ids.shape, -1, jnp.int32)
    for kind in range(2):
        member = ((expert_ids == expert) & (modality == kind)).astype(jnp.int32)
        rank = jnp.cumsum(member, dtype=jnp.int32) - 1
        limit = tile_counts[kind, expert] * TILE
        keep = (member == 1) & (rank < limit)
        places = jnp.where(keep, kind * capacity + rank, places)
    return places


def swap(values, axis, step):
    size = lax.axis_size(axis)
    return lax.ppermute(values, axis, [(i, i ^ step) for i in range(size)])


def bit_half(values, axis, bits, bit, value):
    shape = values.shape
    n = shape[axis]
    low = 2**bit
    split = shape[:axis] + (n // (2 * low), 2, low) + shape[axis + 1 :]
    part = lax.index_in_dim(values.reshape(split), value, axis + 1, keepdims=False)
    return part.reshape(shape[:axis] + (n // 2,) + shape[axis + 1 :])


def bit_join(first, second, axis, bit):
    shape = first.shape
    n = shape[axis]
    low = 2**bit
    split = shape[:axis] + (n // low, 1, low) + shape[axis + 1 :]
    both = jnp.concatenate([first.reshape(split), second.reshape(split)], axis=axis + 1)
    return both.reshape(shape[:axis] + (2 * n,) + shape[axis + 1 :])


def halve(local, weight, order):
    n = local.shape[1]

    def dot(rows):
        flat = rows.reshape(-1, rows.shape[-1])
        out = jnp.dot(flat, weight, preferred_element_type=jnp.float32)
        return out.reshape(rows.shape[:-1] + (weight.shape[1],))

    bit = order[0]
    away = dot(bit_half(local, 1, 0, bit, 1)).astype(jnp.bfloat16)
    came = swap(away, "row", 2**bit)
    total = dot(bit_half(local, 1, 0, bit, 0)) + came.astype(jnp.float32)
    done = [bit]
    for bit in order[1:]:
        at = bit - sum(1 for d in done if d < bit)
        away = bit_half(total, 1, 0, at, 1).astype(jnp.bfloat16)
        came = swap(away, "row", 2**bit)
        total = bit_half(total, 1, 0, at, 0) + came.astype(jnp.float32)
        done.append(bit)
    return total


def spread(values, order):
    done = []
    for bit in order:
        came = swap(values, "row", 2**bit)
        at = sum(1 for d in done if d < bit)
        values = bit_join(values, came, 1, at)
        done.append(bit)
    return values


def per_device(
    tokens,
    expert_ids,
    modality,
    tile_counts,
    router,
    w_gate,
    w_up,
    w_down,
    shared_gate,
    shared_up,
    shared_down,
):
    n_row, n_col = lax.axis_size("row"), lax.axis_size("col")
    bits = n_row.bit_length() - 1
    assert n_row == 2**bits and n_col == 2 * n_row
    row, col = lax.axis_index("row"), lax.axis_index("col")
    core, chip = col & 1, col >> 1
    half = tokens.shape[0] // 2
    width = shared_down.shape[1]
    model = tokens.shape[1]

    def piece(which, start, block):
        return lax.dynamic_slice(tokens, (start, block * width), (half, width))

    mine, other = core * half, (1 - core) * half
    fetched = [swap(piece(0, mine, row ^ s), "row", s) for s in range(1, n_row)]
    near = jnp.stack([piece(0, mine, row)] + fetched)
    crossed = swap(near[1:], "col", 1)
    far = jnp.concatenate([piece(1, other, row)[None], crossed])
    local = jnp.stack([near, far])

    places = slot_places(expert_ids, modality, tile_counts, col)
    index = jnp.arange(2 * n_row)
    chunk = ((row ^ (index % n_row)) * 2) + (core ^ (index // n_row))
    places = places.reshape(2 * n_row, half)[chunk].reshape(-1)
    slots = lax.broadcasted_iota(jnp.int32, (2 * MAXT * TILE, places.shape[0]), 0)
    table = (slots == places[None, :]).astype(jnp.bfloat16)

    flat = local.reshape(-1, width)
    taken_part = jnp.dot(table, flat, preferred_element_type=jnp.float32).astype(jnp.bfloat16)
    taken = jnp.zeros((taken_part.shape[0], model), jnp.bfloat16)
    taken = lax.dynamic_update_slice(taken, taken_part, (0, row * width))
    for s in range(1, n_row):
        came = swap(taken_part, "row", s)
        taken = lax.dynamic_update_slice(taken, came, (0, (row ^ s) * width))

    gate_sum = halve(local, shared_gate, list(range(bits)))
    up_sum = halve(local, shared_up, list(range(bits))[::-1])

    score = jax.nn.sigmoid(jnp.dot(taken, router, preferred_element_type=jnp.float32))
    scaled = (taken.astype(jnp.float32) * score).astype(jnp.bfloat16)
    gate = jnp.dot(scaled, w_gate[0], preferred_element_type=jnp.float32)
    upper = jnp.dot(scaled, w_up[0], preferred_element_type=jnp.float32)
    hidden = (jax.nn.silu(gate) * upper).astype(jnp.bfloat16)
    result = jnp.dot(hidden, w_down[0], preferred_element_type=jnp.float32)

    def columns(block):
        return lax.dynamic_slice_in_dim(result, block * width, width, 1)

    slot_total = columns(row)
    for s in range(1, n_row):
        came = swap(columns(row ^ s).astype(jnp.bfloat16), "row", s)
        slot_total = slot_total + came.astype(jnp.float32)

    shared_hidden = (jax.nn.silu(gate_sum) * up_sum).astype(jnp.bfloat16)
    units = shared_hidden.shape[-1]
    first = spread(shared_hidden[..., : units // 2], list(range(bits))[::-1])
    second = spread(shared_hidden[..., units // 2 :], list(range(bits)))
    spread_hidden = jnp.concatenate([first, second], axis=-1).reshape(-1, units)

    high = slot_total.astype(jnp.bfloat16)
    low = (slot_total - high.astype(jnp.float32)).astype(jnp.bfloat16)
    pair = jnp.concatenate([high, low])
    double = jnp.concatenate([table, table])
    split = spread_hidden.shape[0] // 2

    def combined(start):
        rows = spread_hidden[start : start + split]
        part = jnp.dot(rows, shared_down, preferred_element_type=jnp.float32)
        put = double[:, start : start + split]
        return part + lax.dot_general(
            put, pair, (((0,), (0,)), ((), ())), preferred_element_type=jnp.float32
        )

    came = swap(combined(split).astype(jnp.bfloat16), "col", 1)
    total = (combined(0) + came.astype(jnp.float32)).reshape(n_row, half, width)
    order = (row ^ chip) ^ jnp.arange(n_row)
    blocks = [lax.dynamic_index_in_dim(total, order[u], 0, False) for u in range(n_row)]
    for bit in range(bits):
        away = jnp.stack(blocks[1::2]).astype(jnp.bfloat16)
        came = swap(away, "col", 2 ** (bit + 1))
        blocks = [b + came[i].astype(jnp.float32) for i, b in enumerate(blocks[0::2])]
    return blocks[0].astype(jnp.bfloat16)


def solution(mesh):
    in_specs = (
        P("row", None),
        P(),
        P(),
        P(),
        P(None, "col"),
        P("col", None, "row"),
        P("col", None, "row"),
        P("col", "row", None),
        P("row", "col"),
        P("row", "col"),
        P("col", "row"),
    )
    out_specs = P("col", "row")
    return jax.shard_map(
        per_device, mesh=mesh, in_specs=in_specs, out_specs=out_specs, check_vma=False
    )
```

```python
import functools

import jax
import jax.numpy as jnp
from jax import lax
from jax.experimental import pallas as pl
from jax.experimental.pallas import tpu as pltpu
from jax.sharding import PartitionSpec as P

TILE = 8
MAXT = 4


def table_kernel(n_row, half, where, counts, ids_ref, kinds_ref, in_ref, out_ref):
    row, col = where[0], where[1]
    count = ids_ref.shape[1]
    capacity = MAXT * TILE
    at = lax.broadcasted_iota(jnp.int32, (1, count), 1)
    index = at // half
    before = lax.broadcasted_iota(jnp.int32, (count, count), 0)
    ids, kinds = ids_ref[...], kinds_ref[...]
    members = []
    for kind in range(2):
        member = jnp.where((ids == col) & (kinds == kind), 1.0, 0.0)
        members.append(jnp.broadcast_to(member, (8, count)).astype(jnp.bfloat16))
    for base, table_ref in ((row, in_ref), (col >> 1, out_ref)):
        chunk = (base ^ (index % n_row)) * 2 + ((col & 1) ^ (index // n_row))
        token = chunk * half + at % half
        earlier = jnp.where(before < token, 1.0, 0.0).astype(jnp.bfloat16)
        same = jnp.where(before == token, 1.0, 0.0).astype(jnp.bfloat16)
        places = jnp.full((1, count), -1, jnp.int32)
        for kind in range(2):
            rank = jnp.dot(members[kind], earlier, preferred_element_type=jnp.float32)[:1]
            here = jnp.dot(members[kind], same, preferred_element_type=jnp.float32)[:1]
            rank = rank.astype(jnp.int32)
            keep = (here > 0.5) & (rank < counts[kind, col] * TILE)
            places = jnp.where(keep, kind * capacity + rank, places)
        slots = lax.broadcasted_iota(jnp.int32, (2 * capacity, count), 0)
        table = jnp.where(slots == places, 1.0, 0.0).astype(jnp.bfloat16)
        for start in range(0, table_ref.shape[0], 2 * capacity):
            table_ref[pl.ds(start, 2 * capacity), :] = table


def slot_tables(expert_ids, modality, tile_counts, row, col, n_row, half):
    count = expert_ids.shape[0]
    slots = 2 * MAXT * TILE
    smem = pl.BlockSpec(memory_space=pltpu.SMEM)
    vmem = pl.BlockSpec(memory_space=pltpu.VMEM)
    return pl.pallas_call(
        functools.partial(table_kernel, n_row, half),
        out_shape=[
            jax.ShapeDtypeStruct((slots, count), jnp.bfloat16),
            jax.ShapeDtypeStruct((2 * slots, count), jnp.bfloat16),
        ],
        in_specs=[smem, smem, vmem, vmem],
        out_specs=[vmem, vmem],
        name="slot_tables",
        cost_estimate=pl.CostEstimate(
            flops=64 * count * count, bytes_accessed=8 * count, transcendentals=0
        ),
    )(jnp.stack([row, col]), tile_counts, expert_ids[None], modality[None])


def expert_kernel(x_ref, gate_hbm, up_hbm, down_hbm, out_ref, ring, down, gate_sum, up_sum, sems):
    steps = sems.shape[1]
    slots, depth = ring.shape[1], ring.shape[2]
    wide = down.shape[2]
    loads = []
    for i in range(steps):
        rows = pl.ds(i * depth, depth)
        loads.append(
            [
                pltpu.make_async_copy(hbm.at[0, rows], ring.at[k, i % slots], sems.at[k, i])
                for k, hbm in enumerate((gate_hbm, up_hbm))
            ]
        )
    for i in range(steps):
        columns = pl.ds(i * wide, wide)
        loads.append([pltpu.make_async_copy(down_hbm.at[0, :, columns], down.at[i], sems.at[2, i])])

    def start(i):
        for load in loads[i]:
            load.start()

    for i in range(slots):
        start(i)
    for i in range(steps):
        x = x_ref[:, pl.ds(i * depth, depth)]
        for k, total in enumerate((gate_sum, up_sum)):
            loads[i][k].wait()
            part = jnp.dot(x, ring[k, i % slots], preferred_element_type=jnp.float32)
            total[...] = part if i == 0 else total[...] + part
        if i + slots < steps:
            start(i + slots)
        else:
            first = steps + 2 * (i + slots - steps)
            for j in range(first, min(first + 2, 2 * steps)):
                start(j)
    for j in range(steps + 2 * slots, 2 * steps):
        start(j)
    value = gate_sum[...]
    hidden = (value / (1.0 + jnp.exp(-value)) * up_sum[...]).astype(jnp.bfloat16)
    for i in range(steps):
        loads[steps + i][0].wait()
        columns = pl.ds(i * wide, wide)
        out_ref[:, columns] = jnp.dot(hidden, down[i], preferred_element_type=jnp.float32)


def expert(scaled, w_gate, w_up, w_down):
    slots, model = scaled.shape
    units = w_gate.shape[2]
    steps = 5
    assert model % (steps * 128) == 0
    vmem = pl.BlockSpec(memory_space=pltpu.VMEM)
    whole = pl.BlockSpec(memory_space=pl.ANY)
    return pl.pallas_call(
        expert_kernel,
        out_shape=jax.ShapeDtypeStruct((slots, model), jnp.float32),
        in_specs=[vmem, whole, whole, whole],
        out_specs=vmem,
        scratch_shapes=[
            pltpu.VMEM((2, 3, model // steps, units), jnp.bfloat16),
            pltpu.VMEM((steps, units, model // steps), jnp.bfloat16),
            pltpu.VMEM((slots, units), jnp.float32),
            pltpu.VMEM((slots, units), jnp.float32),
            pltpu.SemaphoreType.DMA((3, steps)),
        ],
        name="routed_expert",
        compiler_params=pltpu.CompilerParams(vmem_limit_bytes=29 * 2**20),
        cost_estimate=pl.CostEstimate(
            flops=6 * slots * model * units,
            bytes_accessed=6 * model * units,
            transcendentals=slots * units,
        ),
    )(scaled, w_gate, w_up, w_down)


def swap(values, axis, step):
    size = lax.axis_size(axis)
    return lax.ppermute(values, axis, [(i, i ^ step) for i in range(size)])


def bit_half(values, axis, bit, value):
    shape = values.shape
    n = shape[axis]
    low = 2**bit
    split = shape[:axis] + (n // (2 * low), 2, low) + shape[axis + 1 :]
    part = lax.index_in_dim(values.reshape(split), value, axis + 1, keepdims=False)
    return part.reshape(shape[:axis] + (n // 2,) + shape[axis + 1 :])


def bit_join(first, second, axis, bit):
    shape = first.shape
    n = shape[axis]
    low = 2**bit
    split = shape[:axis] + (n // low, 1, low) + shape[axis + 1 :]
    both = jnp.concatenate([first.reshape(split), second.reshape(split)], axis=axis + 1)
    return both.reshape(shape[:axis] + (2 * n,) + shape[axis + 1 :])


def halve_first(local, weight, bit):
    def dot(rows):
        flat = rows.reshape(-1, rows.shape[-1])
        out = jnp.dot(flat, weight, preferred_element_type=jnp.float32)
        return out.reshape(rows.shape[:-1] + (weight.shape[1],))

    away = dot(bit_half(local, 1, bit, 1)).astype(jnp.bfloat16)
    came = swap(away, "row", 2**bit)
    kept = dot(bit_half(local, 1, bit, 0))
    return lax.optimization_barrier(kept), came


def halve_rest(kept, came, order):
    total = kept + came.astype(jnp.float32)
    done = [order[0]]
    for bit in order[1:]:
        at = bit - sum(1 for d in done if d < bit)
        away = bit_half(total, 1, at, 1).astype(jnp.bfloat16)
        came = swap(away, "row", 2**bit)
        total = bit_half(total, 1, at, 0) + came.astype(jnp.float32)
        done.append(bit)
    return total


def spread(values, order):
    done = []
    for bit in order:
        came = swap(values, "row", 2**bit)
        at = sum(1 for d in done if d < bit)
        values = bit_join(values, came, 1, at)
        done.append(bit)
    return values


def per_device(
    tokens,
    expert_ids,
    modality,
    tile_counts,
    router,
    w_gate,
    w_up,
    w_down,
    shared_gate,
    shared_up,
    shared_down,
):
    n_row, n_col = lax.axis_size("row"), lax.axis_size("col")
    bits = n_row.bit_length() - 1
    assert n_row == 2**bits and n_col == 2 * n_row
    row, col = lax.axis_index("row"), lax.axis_index("col")
    chip = col >> 1
    half = tokens.shape[0] // 2
    width = shared_down.shape[1]
    model = tokens.shape[1]

    def piece(block, top, source):
        return lax.dynamic_slice(source, (top, block * width), (half, width))

    mine, other = (col & 1) * half, (1 - (col & 1)) * half
    sent = [piece(row ^ s, mine, tokens) for s in range(1, n_row)]
    again, *sent = lax.optimization_barrier((tokens, *sent))
    fetched = [swap(part, "row", s + 1) for s, part in enumerate(sent)]
    crossed = [swap(f, "col", 1) for f in fetched]
    near = jnp.stack([piece(row, mine, again)] + fetched)
    far = jnp.stack([piece(row, other, again)] + crossed)
    local = jnp.stack([near, far])
    table, placing = slot_tables(expert_ids, modality, tile_counts, row, col, n_row, half)

    flat = local.reshape(-1, width)
    taken_part = jnp.dot(table, flat, preferred_element_type=jnp.float32).astype(jnp.bfloat16)
    taken = jnp.zeros((taken_part.shape[0], model), jnp.bfloat16)
    taken = lax.dynamic_update_slice(taken, taken_part, (0, row * width))
    for s in range(1, n_row):
        came = swap(taken_part, "row", s)
        taken = lax.dynamic_update_slice(taken, came, (0, (row ^ s) * width))

    upward, downward = list(range(bits)), list(range(bits))[::-1]
    gate_kept, gate_came = halve_first(local, shared_gate, upward[0])
    up_kept, up_came = halve_first(local, shared_up, downward[0])

    score = jax.nn.sigmoid(jnp.dot(taken, router, preferred_element_type=jnp.float32))
    scaled = (taken.astype(jnp.float32) * score).astype(jnp.bfloat16)
    result = expert(scaled, w_gate, w_up, w_down)
    gate_came, up_came, result = lax.optimization_barrier((gate_came, up_came, result))
    gate_sum = halve_rest(gate_kept, gate_came, upward)
    up_sum = halve_rest(up_kept, up_came, downward)

    def columns(block):
        return lax.dynamic_slice_in_dim(result, block * width, width, 1)

    slot_total = columns(row)
    for s in range(1, n_row):
        leaving = columns(row ^ s).astype(jnp.bfloat16)
        came = swap(leaving, "row", s)
        slot_total = slot_total + came.astype(jnp.float32)

    shared_hidden = (jax.nn.silu(gate_sum) * up_sum).astype(jnp.bfloat16)
    units = shared_hidden.shape[-1]
    first = spread(shared_hidden[..., : units // 2], downward)
    second = spread(shared_hidden[..., units // 2 :], upward)
    whole = jnp.concatenate([first, second], axis=-1)
    ordered = [lax.dynamic_index_in_dim(whole, row ^ chip ^ u, 1, False) for u in range(n_row)]
    outgoing = jnp.stack(ordered, axis=1).reshape(-1, units)

    high = slot_total.astype(jnp.bfloat16)
    low = (slot_total - high.astype(jnp.float32)).astype(jnp.bfloat16)
    pair = jnp.concatenate([high, low])
    split = outgoing.shape[0] // 2

    lanes = width // 2

    def combined(start, left):
        rows = outgoing[start : start + split]
        down = shared_down[:, left : left + lanes]
        part = jnp.dot(rows, down, preferred_element_type=jnp.float32)
        put = placing[:, start : start + split]
        return part + lax.dot_general(
            put,
            pair[:, left : left + lanes],
            (((0,), (0,)), ((), ())),
            preferred_element_type=jnp.float32,
        )

    streams = []
    for left in (0, lanes):
        came = swap(combined(split, left).astype(jnp.bfloat16), "col", 1)
        kept = lax.optimization_barrier(combined(0, left))
        total = (kept + came.astype(jnp.float32)).reshape(n_row, half, lanes)
        streams.append([total[u] for u in range(n_row)])
    for bit in range(bits):
        for i, blocks in enumerate(streams):
            away = jnp.stack(blocks[1::2]).astype(jnp.bfloat16)
            came = swap(away, "col", 2 ** (bit + 1))
            streams[i] = [b + came[j].astype(jnp.float32) for j, b in enumerate(blocks[0::2])]
    return jnp.concatenate([blocks[0] for blocks in streams], axis=1).astype(jnp.bfloat16)


def solution(mesh):
    in_specs = (
        P("row", None),
        P(),
        P(),
        P(),
        P(None, "col"),
        P("col", None, "row"),
        P("col", None, "row"),
        P("col", "row", None),
        P("row", "col"),
        P("row", "col"),
        P("col", "row"),
    )
    out_specs = P("col", "row")
    return jax.shard_map(
        per_device, mesh=mesh, in_specs=in_specs, out_specs=out_specs, check_vma=False
    )
```

```python
import functools

import jax
import jax.numpy as jnp
from jax import lax
from jax.experimental import pallas as pl
from jax.experimental.pallas import tpu as pltpu
from jax.sharding import PartitionSpec as P

TILE = 8
MAXT = 4


def table_kernel(n_row, half, where, counts, ids_ref, kinds_ref, in_ref, out_ref):
    row, col = where[0], where[1]
    count = ids_ref.shape[1]
    capacity = MAXT * TILE
    at = lax.broadcasted_iota(jnp.int32, (1, count), 1)
    index = at // half
    before = lax.broadcasted_iota(jnp.int32, (count, count), 0)
    ids, kinds = ids_ref[...], kinds_ref[...]
    members = []
    for kind in range(2):
        member = jnp.where((ids == col) & (kinds == kind), 1.0, 0.0)
        members.append(jnp.broadcast_to(member, (8, count)).astype(jnp.bfloat16))
    for base, table_ref in ((row, in_ref), (col >> 1, out_ref)):
        chunk = (base ^ (index % n_row)) * 2 + ((col & 1) ^ (index // n_row))
        token = chunk * half + at % half
        earlier = jnp.where(before < token, 1.0, 0.0).astype(jnp.bfloat16)
        same = jnp.where(before == token, 1.0, 0.0).astype(jnp.bfloat16)
        places = jnp.full((1, count), -1, jnp.int32)
        for kind in range(2):
            rank = jnp.dot(members[kind], earlier, preferred_element_type=jnp.float32)[:1]
            here = jnp.dot(members[kind], same, preferred_element_type=jnp.float32)[:1]
            rank = rank.astype(jnp.int32)
            keep = (here > 0.5) & (rank < counts[kind, col] * TILE)
            places = jnp.where(keep, kind * capacity + rank, places)
        slots = lax.broadcasted_iota(jnp.int32, (2 * capacity, count), 0)
        table = jnp.where(slots == places, 1.0, 0.0).astype(jnp.bfloat16)
        for start in range(0, table_ref.shape[0], 2 * capacity):
            table_ref[pl.ds(start, 2 * capacity), :] = table


def slot_tables(expert_ids, modality, tile_counts, row, col, n_row, half):
    count = expert_ids.shape[0]
    slots = 2 * MAXT * TILE
    smem = pl.BlockSpec(memory_space=pltpu.SMEM)
    vmem = pl.BlockSpec(memory_space=pltpu.VMEM)
    return pl.pallas_call(
        functools.partial(table_kernel, n_row, half),
        out_shape=[
            pltpu.VMEM((slots, count), jnp.bfloat16),
            jax.ShapeDtypeStruct((2 * slots, count), jnp.bfloat16),
        ],
        in_specs=[smem, smem, vmem, vmem],
        out_specs=[vmem, vmem],
        name="slot_tables",
        cost_estimate=pl.CostEstimate(
            flops=64 * count * count, bytes_accessed=8 * count, transcendentals=0
        ),
    )(jnp.stack([row, col]), tile_counts, expert_ids[None], modality[None])


def expert_kernel(x_ref, gate_hbm, up_hbm, down_hbm, out_ref, ring, down, gate_sum, up_sum, sems):
    steps = sems.shape[1]
    slots, depth = ring.shape[1], ring.shape[2]
    wide = down.shape[2]
    loads = []
    for i in range(steps):
        rows = pl.ds(i * depth, depth)
        loads.append(
            [
                pltpu.make_async_copy(hbm.at[0, rows], ring.at[k, i % slots], sems.at[k, i])
                for k, hbm in enumerate((gate_hbm, up_hbm))
            ]
        )
    for i in range(steps):
        columns = pl.ds(i * wide, wide)
        loads.append([pltpu.make_async_copy(down_hbm.at[0, :, columns], down.at[i], sems.at[2, i])])

    def start(i):
        for load in loads[i]:
            load.start()

    for i in range(slots):
        start(i)
    for i in range(steps):
        x = x_ref[:, pl.ds(i * depth, depth)]
        for k, total in enumerate((gate_sum, up_sum)):
            loads[i][k].wait()
            part = jnp.dot(x, ring[k, i % slots], preferred_element_type=jnp.float32)
            total[...] = part if i == 0 else total[...] + part
        if i + slots < steps:
            start(i + slots)
        else:
            first = steps + 2 * (i + slots - steps)
            for j in range(first, min(first + 2, 2 * steps)):
                start(j)
    for j in range(steps + 2 * slots, 2 * steps):
        start(j)
    value = gate_sum[...]
    hidden = (value / (1.0 + jnp.exp(-value)) * up_sum[...]).astype(jnp.bfloat16)
    for i in range(steps):
        loads[steps + i][0].wait()
        columns = pl.ds(i * wide, wide)
        out_ref[:, columns] = jnp.dot(hidden, down[i], preferred_element_type=jnp.float32)


def expert(scaled, w_gate, w_up, w_down):
    slots, model = scaled.shape
    units = w_gate.shape[2]
    steps = 5
    assert model % (steps * 128) == 0
    vmem = pl.BlockSpec(memory_space=pltpu.VMEM)
    whole = pl.BlockSpec(memory_space=pl.ANY)
    return pl.pallas_call(
        expert_kernel,
        out_shape=jax.ShapeDtypeStruct((slots, model), jnp.float32),
        in_specs=[vmem, whole, whole, whole],
        out_specs=vmem,
        scratch_shapes=[
            pltpu.VMEM((2, 3, model // steps, units), jnp.bfloat16),
            pltpu.VMEM((steps, units, model // steps), jnp.bfloat16),
            pltpu.VMEM((slots, units), jnp.float32),
            pltpu.VMEM((slots, units), jnp.float32),
            pltpu.SemaphoreType.DMA((3, steps)),
        ],
        name="routed_expert",
        compiler_params=pltpu.CompilerParams(vmem_limit_bytes=29 * 2**20),
        cost_estimate=pl.CostEstimate(
            flops=6 * slots * model * units,
            bytes_accessed=6 * model * units,
            transcendentals=slots * units,
        ),
    )(scaled, w_gate, w_up, w_down)


def act_kernel(gate_ref, gate_more, up_ref, up_more, first_ref, second_ref):
    gate = gate_ref[...] + gate_more[...].astype(jnp.float32)
    upper = up_ref[...] + up_more[...].astype(jnp.float32)
    value = (gate / (1.0 + jnp.exp(-gate)) * upper).astype(jnp.bfloat16)
    units = first_ref.shape[-1]
    first_ref[...] = value[..., :units]
    second_ref[...] = value[..., units:]


def act(gate, gate_more, up, up_more):
    shape = gate_more.shape[:-1] + (gate_more.shape[-1] // 2,)
    vmem = pl.BlockSpec(shape, lambda i: (0, 0, 0, 0))
    front = pl.BlockSpec(gate_more.shape, lambda i: (0, 0, 0, 0))
    return pl.pallas_call(
        act_kernel,
        out_shape=[pltpu.VMEM(shape, jnp.bfloat16)] * 2,
        grid=(1,),
        in_specs=[front] * 4,
        out_specs=[vmem] * 2,
        name="act",
        cost_estimate=pl.CostEstimate(
            flops=8 * gate.size, bytes_accessed=16 * gate.size, transcendentals=gate.size
        ),
    )(gate, gate_more, up, up_more)


def swap(values, axis, step):
    size = lax.axis_size(axis)
    return lax.ppermute(values, axis, [(i, i ^ step) for i in range(size)])


def bit_half(values, axis, bit, value):
    shape = values.shape
    n = shape[axis]
    low = 2**bit
    split = shape[:axis] + (n // (2 * low), 2, low) + shape[axis + 1 :]
    part = lax.index_in_dim(values.reshape(split), value, axis + 1, keepdims=False)
    return part.reshape(shape[:axis] + (n // 2,) + shape[axis + 1 :])


def bit_join(first, second, axis, bit):
    shape = first.shape
    n = shape[axis]
    low = 2**bit
    split = shape[:axis] + (n // low, 1, low) + shape[axis + 1 :]
    both = jnp.concatenate([first.reshape(split), second.reshape(split)], axis=axis + 1)
    return both.reshape(shape[:axis] + (2 * n,) + shape[axis + 1 :])


def halve_first(local, weight, bit):
    def dot(rows):
        flat = rows.reshape(-1, rows.shape[-1])
        out = jnp.dot(flat, weight, preferred_element_type=jnp.float32)
        return out.reshape(rows.shape[:-1] + (weight.shape[1],))

    away = dot(bit_half(local, 1, bit, 1)).astype(jnp.bfloat16)
    came = swap(away, "row", 2**bit)
    kept = dot(bit_half(local, 1, bit, 0))
    return lax.optimization_barrier(kept), came


def halve_rest(kept, came, order):
    done = [order[0]]
    for bit in order[1:]:
        total = kept + came.astype(jnp.float32)
        at = bit - sum(1 for d in done if d < bit)
        away = bit_half(total, 1, at, 1).astype(jnp.bfloat16)
        came = swap(away, "row", 2**bit)
        kept = total if bit == order[-1] else bit_half(total, 1, at, 0)
        done.append(bit)
    return kept, came


def spread(values, order):
    done = []
    for bit in order:
        came = swap(values, "row", 2**bit)
        at = sum(1 for d in done if d < bit)
        values = bit_join(values, came, 1, at)
        done.append(bit)
    return values


def per_device(
    tokens,
    expert_ids,
    modality,
    tile_counts,
    router,
    w_gate,
    w_up,
    w_down,
    shared_gate,
    shared_up,
    shared_down,
):
    n_row, n_col = lax.axis_size("row"), lax.axis_size("col")
    bits = n_row.bit_length() - 1
    assert n_row == 2**bits and n_col == 2 * n_row
    row, col = lax.axis_index("row"), lax.axis_index("col")
    chip = col >> 1
    half = tokens.shape[0] // 2
    width = shared_down.shape[1]
    model = tokens.shape[1]

    def piece(block, top, source):
        return lax.dynamic_slice(source, (top, block * width), (half, width))

    mine, other = (col & 1) * half, (1 - (col & 1)) * half
    sent = [piece(row ^ s, mine, tokens) for s in range(1, n_row)]
    again, *sent = lax.optimization_barrier((tokens, *sent))
    fetched = [swap(part, "row", s + 1) for s, part in enumerate(sent)]
    crossed = [swap(f, "col", 1) for f in fetched]
    near = jnp.stack([piece(row, mine, again)] + fetched)
    far = jnp.stack([piece(row, other, again)] + crossed)
    local = jnp.stack([near, far])
    table, placing = slot_tables(expert_ids, modality, tile_counts, row, col, n_row, half)

    flat = local.reshape(-1, width)
    taken_part = jnp.dot(table, flat, preferred_element_type=jnp.float32).astype(jnp.bfloat16)
    taken = jnp.zeros((taken_part.shape[0], model), jnp.bfloat16)
    taken = lax.dynamic_update_slice(taken, taken_part, (0, row * width))
    for s in range(1, n_row):
        came = swap(taken_part, "row", s)
        taken = lax.dynamic_update_slice(taken, came, (0, (row ^ s) * width))

    upward, downward = list(range(bits)), list(range(bits))[::-1]
    gate_kept, gate_came = halve_first(local, shared_gate, upward[0])
    up_kept, up_came = halve_first(local, shared_up, downward[0])

    score = jax.nn.sigmoid(jnp.dot(taken, router, preferred_element_type=jnp.float32))
    scaled = (taken.astype(jnp.float32) * score).astype(jnp.bfloat16)
    result = expert(scaled, w_gate, w_up, w_down)
    gate_came, up_came, result = lax.optimization_barrier((gate_came, up_came, result))
    gate_sum = halve_rest(gate_kept, gate_came, upward)
    up_sum = halve_rest(up_kept, up_came, downward)

    def columns(block):
        return lax.dynamic_slice_in_dim(result, block * width, width, 1)

    slot_total = columns(row)
    for s in range(1, n_row):
        leaving = columns(row ^ s).astype(jnp.bfloat16)
        came = swap(leaving, "row", s)
        slot_total = slot_total + came.astype(jnp.float32)

    units = shared_gate.shape[1]
    first, second = act(*gate_sum, *up_sum)
    first = spread(first, downward)
    second = spread(second, upward)
    whole = jnp.concatenate([first, second], axis=-1)
    ordered = [lax.dynamic_index_in_dim(whole, row ^ chip ^ u, 1, False) for u in range(n_row)]
    outgoing = jnp.stack(ordered, axis=1).reshape(-1, units)

    high = slot_total.astype(jnp.bfloat16)
    low = (slot_total - high.astype(jnp.float32)).astype(jnp.bfloat16)
    pair = jnp.concatenate([high, low])
    split = outgoing.shape[0] // 2

    lanes = width // 2

    def down(start):
        rows = outgoing[start : start + split]
        return jnp.dot(rows, shared_down, preferred_element_type=jnp.float32)

    def placed(start, left):
        return lax.dot_general(
            placing[:, start : start + split],
            pair[:, left : left + lanes],
            (((0,), (0,)), ((), ())),
            preferred_element_type=jnp.float32,
        )

    lefts = (0, lanes)
    leaving, staying = down(split), down(0)
    moved = [(leaving[:, i : i + lanes] + placed(split, i)).astype(jnp.bfloat16) for i in lefts]
    moved = [swap(part, "col", 1) for part in moved]
    streams = []
    for left, came in zip(lefts, moved):
        kept = lax.optimization_barrier(staying[:, left : left + lanes] + placed(0, left))
        total = (kept + came.astype(jnp.float32)).reshape(n_row, half, lanes)
        streams.append([total[u] for u in range(n_row)])
    for bit in range(bits):
        for i, blocks in enumerate(streams):
            away = jnp.stack(blocks[1::2]).astype(jnp.bfloat16)
            came = swap(away, "col", 2 ** (bit + 1))
            streams[i] = [b + came[j].astype(jnp.float32) for j, b in enumerate(blocks[0::2])]
    return jnp.concatenate([blocks[0] for blocks in streams], axis=1).astype(jnp.bfloat16)


def solution(mesh):
    in_specs = (
        P("row", None),
        P(),
        P(),
        P(),
        P(None, "col"),
        P("col", None, "row"),
        P("col", None, "row"),
        P("col", "row", None),
        P("row", "col"),
        P("row", "col"),
        P("col", "row"),
    )
    out_specs = P("col", "row")
    return jax.shard_map(
        per_device, mesh=mesh, in_specs=in_specs, out_specs=out_specs, check_vma=False
    )
```
